32 devices in a mesh: groups: 2 (over y), row: 4 (over x, core), col: 4 (over z).
Axes of the slice: x: 2, y: 2, z: 4, core: 2. Of those that a mesh axis runs over, the one named last changes fastest.
Arguments:
- slope_matrix: bfloat16 [1024, 1024], P(('groups', 'row'), 'col'), parts along dimension 0, may hold values from -0.3125 to 0.3125
- prior_matrix: bfloat16 [1024, 1024], P(('groups', 'row'), 'col'), parts along dimension 0, may hold values from -0.3125 to 0.3125
- slope_blocks: int32 [8, 8], P(('groups', 'row'), 'col'), parts along dimension 0, may hold values from 0 to 23, as said below
- prior_blocks: int32 [8, 8], P(('groups', 'row'), 'col'), parts along dimension 0, may hold values from 0 to 23, as said below
- weight_ids: int32 [512], P(('groups', 'row')), parts along dimension 0, may hold values from 0 to 15
- valid_mask: int32 [512], P(('groups', 'row')), parts along dimension 0, may hold values 0 or 1
- noise_weights: float32 [32], P('groups'), parts along dimension 0, may hold values from 0.25 to 4
- prior_weights: bfloat16 [1024], P(('groups', 'row')), parts along dimension 0, may hold values from 0.19921875 to 2
- frames: float32 [6144, 64], P(('groups', 'row', 'col')), parts along dimension 0, may hold values from -6 to 6
Outputs:
- gram_matrix: float32 [6144, 3072], P(('groups', 'row'), 'col'), parts along dimension 0
- applied: float32 [6144, 64], P(('groups', 'row', 'col')), parts along dimension 0
The draws below stay inside these ranges and needn't reach their ends.
There are 2 independent parts, one for each index of `groups`. The reference program is written for one: setup_inputs(seed, part) draws one part's arguments, and reference() takes and returns one part's arrays. A program takes and returns all parts, laid end to end along the dimension named above; each array names one. Nothing has to cross between parts.
Inputs may be any that keep to these rules, and one draw needn't show every extreme that they name: `slope_blocks`: row i names, for each block-column set c (entries c * 2 to c * 2 + 1), 2 distinct actuator blocks of that set, c * 6 to c * 6 + 5, in the order in which their blocks are stored. `prior_blocks`: row i names, for each block-column set c (entries c * 2 to c * 2 + 1), 2 distinct actuator blocks of that set, c * 6 to c * 6 + 5, in the order in which their blocks are stored.
All inputs are finite; a program needn't handle non-finite values. No bound on the sum of `valid_mask` on one device may be relied on, other than what follows from the above.
Results may differ from the reference program's by a relative error of at most 0.007.
Values may be sent and summed in bfloat16 or wider, within the bound.
No kernel may reach another device: no remote copies, remote signals or barrier semaphores. Data moves between devices by JAX's collectives and lax.ppermute only.
A program may use at most 128 MiB of HBM per device.

```python
import math
import jax
import jax.numpy as jnp
from jax import lax

BS = 128
AB = 6
KD = 2
SB = 1
PB = 1
F = 64
NW = 16
NA = 24
NS = 512
NP = 512
NSUB = 256
N_ROW = 4
N_COL = 4


def draw_blocks(key, block_rows):
    scores = jax.random.randint(key, (block_rows, N_COL, AB), 1, 1 << 20)
    local = jnp.arange(AB, dtype=jnp.int32)
    first_row = (jnp.arange(block_rows, dtype=jnp.int32) == 0)[:, None, None]
    end_blocks = ((local == 0) | (local == AB - 1))[None, None, :]
    scores = jnp.where(first_row & end_blocks, 0, scores)
    keyed = scores * AB + local[None, None, :]
    ordering = jnp.argsort(keyed, axis=2)
    chosen = ordering[:, :, :KD].astype(jnp.int32)
    set_start = jnp.arange(N_COL, dtype=jnp.int32)[None, :, None] * AB
    return (chosen + set_start).reshape(block_rows, N_COL * KD)


def draw_slope_blocks(key, part):
    return draw_blocks(jax.random.fold_in(key, 3), SB * N_ROW)


def draw_prior_blocks(key, part):
    return draw_blocks(jax.random.fold_in(key, 7), PB * N_ROW)


def touch_ends(result, own_key, smallest, high):
    shape = result.shape
    place = [jax.random.randint(jax.random.fold_in(own_key, axis), (), 0, shape[axis]) for axis in range(len(shape))]
    result = result.at[tuple(place)].set(smallest)
    longest = shape.index(max(shape))
    place[longest] = (place[longest] + 1) % shape[longest]
    return result.at[tuple(place)].set(high)


def shard_levels(own_key, dims, shards, smallest, largest):
    loudness, own = 1.0, jax.random.fold_in(own_key, 6)
    for dim, shards_of in shards:
        draws = jnp.exp(jax.random.uniform(jax.random.fold_in(own, dim), (shards_of,), jnp.float32, smallest / len(shards), largest / len(shards)))
        loudness = loudness * jnp.repeat(draws, dims[dim] // shards_of).reshape([-1 if axis == dim else 1 for axis in range(len(dims))])
    return loudness


def bell_draw(key, shape, spread, bound, shards=(), kind=jnp.bfloat16):
    array = jax.random.normal(key, shape, jnp.float32) * spread
    if len(shards) > 0:
        array = shard_levels(key, shape, shards, -0.22, 0.18) * array
    return jnp.clip(array, min=-bound, max=bound).astype(kind)


def setup_inputs(seed: int = 0, part: int = 0) -> dict:
    key_of = jax.random.split(jax.random.key(seed), 10)
    part_splits = jax.random.split(jax.random.fold_in(key_of[9], part), 10)
    slope_matrix = bell_draw(part_splits[0], (NS, N_COL * KD * BS), (N_ROW * (SB + PB) * BS * KD // AB) ** -0.5, 0.3125, ((0, 4), (1, 4)))
    prior_matrix = bell_draw(part_splits[1], (NP, N_COL * KD * BS), (N_ROW * (SB + PB) * BS * KD // AB) ** -0.5, 0.3125, ((0, 4), (1, 4)))
    slope_blocks = draw_slope_blocks(jax.random.fold_in(jax.random.fold_in(key_of[9], part), 71), part)
    prior_blocks = draw_prior_blocks(jax.random.fold_in(jax.random.fold_in(key_of[9], part), 71), part)
    weight_ids = touch_ends(jax.random.randint(part_splits[4], (NSUB,), 0, NW), jax.random.fold_in(part_splits[4], 1), 0, NW - 1).astype(jnp.int32)
    valid_mask = touch_ends((jax.random.randint(part_splits[5], (NSUB,), 0, 4) < 3).astype(jnp.int32), jax.random.fold_in(part_splits[5], 1), 0, 1)
    noise_weights = jnp.clip(jnp.exp(jax.random.uniform(part_splits[6], (NW,), jnp.float32, math.log(0.25), math.log(4.0))), 0.25, 4.0)
    prior_weights = jnp.clip(jnp.exp(math.log(2.0) - 2.306499 * jax.random.uniform(part_splits[7], (NP,), jnp.float32) ** shard_levels(part_splits[7], (NP,), ((0, 4),), -0.2, 0.2)), 0.19921875, 2.0).astype(jnp.bfloat16)
    frames = bell_draw(part_splits[8], (NA * BS, F), 1.0, 6.0, ((0, 16),), jnp.float32)
    return dict(slope_matrix=slope_matrix, prior_matrix=prior_matrix, slope_blocks=slope_blocks, prior_blocks=prior_blocks, weight_ids=weight_ids, valid_mask=valid_mask, noise_weights=noise_weights, prior_weights=prior_weights, frames=frames)


def expand_all(values, block_ids):
    block_count = block_ids.shape[0]
    chosen = block_ids.shape[1]
    targets = jnp.arange(NA, dtype=jnp.int32)
    onehot = (block_ids[:, :, None] == targets[None, None, :]).astype(jnp.float32)
    shaped = values.astype(jnp.float32).reshape(block_count, BS, chosen, BS)
    expanded = jnp.einsum("rskb,rka->rsab", shaped, onehot)
    return expanded.reshape(block_count * BS, NA * BS).astype(jnp.bfloat16)


def reference(slope_matrix, prior_matrix, slope_blocks, prior_blocks, weight_ids, valid_mask, noise_weights, prior_weights, frames):
    subap_weight = noise_weights[weight_ids] * valid_mask.astype(jnp.float32)
    slope_weight = jnp.repeat(subap_weight, 2).astype(jnp.bfloat16)
    slope_dense = expand_all(slope_matrix, slope_blocks)
    prior_dense = expand_all(prior_matrix, prior_blocks)
    slope_weighted = (slope_dense.astype(jnp.float32) * slope_weight.astype(jnp.float32)[:, None]).astype(jnp.bfloat16)
    prior_weighted = (prior_dense.astype(jnp.float32) * prior_weights.astype(jnp.float32)[:, None]).astype(jnp.bfloat16)
    slope_part = jnp.dot(slope_dense.astype(jnp.float32).T, slope_weighted.astype(jnp.float32), preferred_element_type=jnp.float32)
    prior_part = jnp.dot(prior_dense.astype(jnp.float32).T, prior_weighted.astype(jnp.float32), preferred_element_type=jnp.float32)
    gram_matrix = slope_part + prior_part
    applied = jnp.dot(gram_matrix, frames, precision=lax.Precision.HIGHEST, preferred_element_type=jnp.float32)
    return (gram_matrix, applied)
```

```python
import functools

import jax
import jax.numpy as jnp
from jax import lax
from jax.experimental import pallas as pl
from jax.experimental.pallas import tpu as pltpu
from jax.sharding import PartitionSpec as P


VMEM = pl.BlockSpec(memory_space=pltpu.VMEM)
SMEM = pl.BlockSpec(memory_space=pltpu.SMEM)
F32 = jnp.float32
BF16 = jnp.bfloat16
EXTRA = 16


def permute(value, n, source):
    pairs = []
    for r in range(n):
        for c in range(n):
            sr, sc = source(r, c)
            pairs.append((sr * n + sc, r * n + c))
    return lax.ppermute(value, ("row", "col"), pairs)


def pack_kernel(ab, slope, prior, ids_s, ids_p, wid, valid, pw, noise, frames, packed, sent):
    rows, width = slope.shape
    half = wid.shape[1]
    packed[0:rows, :] = slope[...]
    packed[rows : 2 * rows, :] = prior[...]
    picked = jnp.zeros((1, half), F32)
    for k in range(noise.shape[0]):
        picked = picked + jnp.where(wid[...] == k, noise[k], 0.0)
    picked = picked * valid[...].astype(F32)
    source = lax.broadcasted_iota(jnp.int32, (half, rows), 0)
    target = lax.broadcasted_iota(jnp.int32, (half, rows), 1)
    spread = jnp.where(target // 2 == source, 1.0, 0.0).astype(BF16)
    eight = jnp.broadcast_to(picked, (8, half)).astype(BF16)
    slope_w = jnp.dot(eight, spread, preferred_element_type=F32)[0:1]
    weights = jnp.concatenate([slope_w, pw[...].astype(F32)], axis=1)
    base = lax.axis_index("col") * ab
    row = lax.broadcasted_iota(jnp.int32, (EXTRA, width), 0)
    lane = lax.broadcasted_iota(jnp.int32, (EXTRA, width), 1)
    tile = jnp.where(row == 0, jnp.broadcast_to(weights, (EXTRA, width)), 0.0)
    for line, ids in ((1, ids_s), (2, ids_p)):
        for e in range(ids.shape[1]):
            here = (row == line) & (lane // rows == e)
            tile = jnp.where(here, (ids[0, e] - base).astype(F32), tile)
    packed[2 * rows :, :] = tile.astype(BF16)
    sent[...] = frames[...].astype(BF16)


def info(block, rows, which):
    tile = block[2 * rows :, :].astype(F32)
    weight = tile[0:1, which * rows : (which + 1) * rows]
    numbers = [tile[1 + which : 2 + which, e * rows : (e + 1) * rows] for e in range(tile.shape[1] // rows)]
    return weight, numbers


def image_kernel(n, ab, rows, *refs):
    cols, frames, outs, v, image = refs[:2 * n], refs[2 * n], refs[2 * n + 1 : 3 * n + 1], refs[-2], refs[-1]
    own_c, own_r = cols[:n], cols[n:]
    r, c = lax.axis_index("row"), lax.axis_index("col")
    nf, per = frames.shape[1], frames.shape[2]
    image[...] = jnp.zeros_like(image)
    for k in range(n):
        start = k * per // rows * rows
        shift = k * per - start
        wide = (per + shift + rows - 1) // rows * rows
        piece = jnp.concatenate([frames[k].astype(F32), jnp.zeros((nf, wide - per), F32)], axis=1)
        if shift:
            piece = pltpu.roll(piece, shift, 1)
        image[:, start : start + wide] += piece
    parts = [image[:, b * rows : (b + 1) * rows] for b in range(ab)]
    for k in range(n):
        block = own_c[k]
        place = lax.rem(r + k, n)
        for which in range(2):
            weight, numbers = info(block, rows, which)
            chosen = []
            for number in numbers:
                pick = jnp.zeros((nf, rows), F32)
                for b in range(ab):
                    pick = jnp.where(number == float(b), parts[b], pick)
                chosen.append(pick)
            picked = jnp.concatenate(chosen, axis=1).astype(BF16)
            values = block[which * rows : (which + 1) * rows, :]
            result = lax.dot_general(picked, values, (((1,), (1,)), ((), ())), preferred_element_type=F32)
            result = result * weight
            high = result.astype(BF16)
            low = (result - high.astype(F32)).astype(BF16)
            v[place, which] = jnp.concatenate([high, low], axis=0)
    totals = [jnp.zeros((nf, rows), F32) for _ in range(ab)]
    for k in range(n):
        block = own_r[k]
        place = lax.rem(c + k, n)
        for which in range(2):
            _, numbers = info(block, rows, which)
            values = block[which * rows : (which + 1) * rows, :]
            both = jnp.dot(v[place, which], values, preferred_element_type=F32)
            both = both[:nf] + both[nf:]
            for e, number in enumerate(numbers):
                part = both[:, e * rows : (e + 1) * rows]
                for b in range(ab):
                    totals[b] = totals[b] + jnp.where(number == float(b), part, 0.0)
    for b in range(ab):
        image[:, b * rows : (b + 1) * rows] = totals[b]
    for k in range(n):
        start = k * per // rows * rows
        shift = k * per - start
        wide = (per + shift + rows - 1) // rows * rows
        piece = image[:, start : start + wide]
        if shift:
            piece = pltpu.roll(piece, wide - shift, 1)
        v_slice = piece[:, :per]
        for j in range(n):
            @pl.when(lax.rem(c - k + n, n) == j)
            def _():
                outs[j][...] = v_slice.astype(outs[j].dtype)


def dense_kernel(n, ab, rows, *refs):
    own_c, own_r, left, right = refs[:n], refs[n : 2 * n], refs[2 * n], refs[2 * n + 1]
    r, c = lax.axis_index("row"), lax.axis_index("col")
    eye = lax.broadcasted_iota(jnp.int32, (rows, rows), 0) == lax.broadcasted_iota(jnp.int32, (rows, rows), 1)
    for blocks, out, position, weighted in ((own_c, right, r, True), (own_r, left, c, False)):
        for k in range(n):
            block = blocks[k]
            base = lax.rem(position + k, n) * (2 * rows)
            for which in range(2):
                weight, numbers = info(block, rows, which)
                values = block[which * rows : (which + 1) * rows, :]
                if weighted:
                    scale = jnp.where(eye, jnp.broadcast_to(weight, (rows, rows)), 0.0).astype(BF16)
                    values = jnp.dot(scale, values, preferred_element_type=F32)
                else:
                    values = values.astype(F32)
                at = pl.ds(pl.multiple_of(base + which * rows, rows), rows)
                for b in range(ab):
                    total = jnp.zeros((rows, rows), F32)
                    for e, number in enumerate(numbers):
                        total = jnp.where(number == float(b), values[:, e * rows : (e + 1) * rows], total)
                    out[at, b * rows : (b + 1) * rows] = total.astype(BF16)


def shards(n, slope_matrix, prior_matrix, slope_blocks, prior_blocks, weight_ids, valid_mask, noise_weights, prior_weights, frames):
    rows, width = slope_matrix.shape
    per, nf = frames.shape
    ab = per * n // rows
    shape = jax.ShapeDtypeStruct
    packed, sent = pl.pallas_call(
        functools.partial(pack_kernel, ab),
        out_shape=(shape((2 * rows + EXTRA, width), BF16), shape((nf, per), BF16)),
        in_specs=[VMEM, VMEM, SMEM, SMEM, VMEM, VMEM, VMEM, SMEM, VMEM],
        out_specs=(VMEM, VMEM),
        name="pack",
    )(
        slope_matrix,
        prior_matrix,
        slope_blocks,
        prior_blocks,
        weight_ids[None, :],
        valid_mask[None, :],
        prior_weights[None, :],
        noise_weights,
        frames.T,
    )
    turned = permute(sent, n, lambda r, c: (c, r))
    row_side = [permute(packed, n, lambda r, c, k=k: ((c + k) % n, r)) for k in range(n)]
    col_side = [packed] + [permute(packed, n, lambda r, c, k=k: ((r + k) % n, c)) for k in range(1, n)]
    mine = lax.all_gather(turned, "row", axis=0)
    pieces = pl.pallas_call(
        functools.partial(image_kernel, n, ab, rows),
        out_shape=tuple([shape((nf, per), F32)] + [shape((nf, per), BF16)] * (n - 1)),
        in_specs=[VMEM] * (2 * n + 1),
        out_specs=tuple([VMEM] * n),
        scratch_shapes=[pltpu.VMEM((n, 2, 2 * nf, rows), BF16), pltpu.VMEM((nf, ab * rows), F32)],
        name="image",
    )(*col_side, *row_side, mine)
    got = [permute(pieces[k], n, lambda r, c, k=k: (r, (c + k) % n)) for k in range(1, n)]
    left, right = pl.pallas_call(
        functools.partial(dense_kernel, n, ab, rows),
        out_shape=(shape((2 * rows * n, ab * rows), BF16), shape((2 * rows * n, ab * rows), BF16)),
        in_specs=[VMEM] * (2 * n),
        out_specs=(VMEM, VMEM),
        name="dense",
    )(*col_side, *row_side)
    gram = lax.dot_general(left, right, (((0,), (0,)), ((), ())), preferred_element_type=F32)
    total = pieces[0]
    for piece in got:
        total = total + piece.astype(F32)
    return gram, total.T


def solution(mesh):
    n = mesh.shape["row"]
    block = P(("groups", "row"), "col")
    line = P(("groups", "row"))
    whole = P(("groups", "row", "col"), None)
    in_specs = (block, block, block, block, line, line, P("groups"), line, whole)
    return jax.shard_map(
        functools.partial(shards, n), mesh=mesh, in_specs=in_specs, out_specs=(block, whole), check_vma=False
    )
```

```python
import functools

import jax
import jax.numpy as jnp
from jax import lax
from jax.experimental import pallas as pl
from jax.experimental.pallas import tpu as pltpu
from jax.sharding import PartitionSpec as P


VMEM = pl.BlockSpec(memory_space=pltpu.VMEM)
SMEM = pl.BlockSpec(memory_space=pltpu.SMEM)
F32 = jnp.float32
BF16 = jnp.bfloat16
EXTRA = 16
SMALL = pltpu.CompilerParams(vmem_limit_bytes=16 << 20)


def here(*values):
    return [pltpu.with_memory_space_constraint(v, pltpu.VMEM) for v in values]


def permute(value, n, source):
    pairs = []
    for r in range(n):
        for c in range(n):
            sr, sc = source(r, c)
            pairs.append((sr * n + sc, r * n + c))
    return lax.ppermute(value, ("row", "col"), pairs)


def pack_kernel(ab, slope, prior, ids_s, ids_p, wid, valid, pw, noise, frames, packed, sent):
    rows, width = slope.shape
    half = wid.shape[1]
    packed[0:rows, :] = slope[...]
    packed[rows : 2 * rows, :] = prior[...]
    picked = jnp.zeros((1, half), F32)
    for k in range(noise.shape[0]):
        picked = picked + jnp.where(wid[...] == k, noise[k], 0.0)
    picked = picked * valid[...].astype(F32)
    source = lax.broadcasted_iota(jnp.int32, (half, rows), 0)
    target = lax.broadcasted_iota(jnp.int32, (half, rows), 1)
    spread = jnp.where(target // 2 == source, 1.0, 0.0).astype(BF16)
    eight = jnp.broadcast_to(picked, (8, half)).astype(BF16)
    slope_w = jnp.dot(eight, spread, preferred_element_type=F32)[0:1]
    weights = jnp.concatenate([slope_w, pw[...].astype(F32)], axis=1)
    base = lax.axis_index("col") * ab
    row = lax.broadcasted_iota(jnp.int32, (EXTRA, width), 0)
    lane = lax.broadcasted_iota(jnp.int32, (EXTRA, width), 1)
    tile = jnp.where(row == 0, jnp.broadcast_to(weights, (EXTRA, width)), 0.0)
    for line, ids in ((1, ids_s), (2, ids_p)):
        for e in range(ids.shape[1]):
            here = (row == line) & (lane // rows == e)
            tile = jnp.where(here, (ids[0, e] - base).astype(F32), tile)
    packed[2 * rows :, :] = tile.astype(BF16)
    nf, per = frames.shape
    sent[...] = jnp.concatenate([frames[...], jnp.zeros((nf, width - per), F32)], axis=1).astype(BF16)


def info(block, rows, which):
    tile = block[2 * rows : 2 * rows + EXTRA, :].astype(F32)
    weight = tile[0:1, which * rows : (which + 1) * rows]
    numbers = [tile[1 + which : 2 + which, e * rows : (e + 1) * rows] for e in range(tile.shape[1] // rows)]
    return weight, numbers


def col_places(n, r):
    return [lax.rem((r ^ odd) + 2 * m, n) for m in range(n // 2) for odd in (0, 1)]


def row_places(n, r, c):
    return [lax.rem((c ^ odd) + 2 * (m + r), n) for odd in (0, 1) for m in range(n // 2)]


def picture_kernel(n, ab, rows, per, *refs):
    blocks, frames, out, image, slices = refs[:n], refs[n : 2 * n], refs[-3], refs[-2], refs[-1]
    r, c = lax.axis_index("row"), lax.axis_index("col")
    nf = frames[0].shape[0]
    for k in range(n):
        slices[lax.rem(c + k, n)] = frames[k][...].astype(F32)
    image[...] = jnp.zeros_like(image)
    for k in range(n):
        start = k * per // rows * rows
        shift = k * per - start
        wide = (per + shift + rows - 1) // rows * rows
        piece = slices[k]
        if shift:
            piece = pltpu.roll(piece, shift, 1)
        image[:, start : start + wide] += piece[:, :wide]
    parts = [image[:, b * rows : (b + 1) * rows] for b in range(ab)]
    for block, place in zip(blocks, row_places(n, r, c)):
        for which in range(2):
            weight, numbers = info(block, rows, which)
            chosen = []
            for number in numbers:
                pick = jnp.zeros((nf, rows), F32)
                for b in range(ab):
                    pick = jnp.where(number == float(b), parts[b], pick)
                chosen.append(pick)
            picked = jnp.concatenate(chosen, axis=1).astype(BF16)
            values = block[which * rows : (which + 1) * rows, :]
            result = lax.dot_general(picked, values, (((1,), (1,)), ((), ())), preferred_element_type=F32)
            out[2 * place + which] = (result * weight).astype(BF16)


def applied_kernel(n, ab, rows, per, *refs):
    blocks, sums, out, image = refs[:n], refs[n : n + n // 2], refs[-2], refs[-1]
    r, c = lax.axis_index("row"), lax.axis_index("col")
    nf = image.shape[0]
    totals = [jnp.zeros((nf, rows), F32) for _ in range(ab)]
    for block, place in zip(blocks, row_places(n, r, c)):
        for which in range(2):
            _, numbers = info(block, rows, which)
            values = block[which * rows : (which + 1) * rows, :]
            result = sums[0][2 * place + which].astype(F32)
            for other in sums[1:]:
                result = result + other[2 * place + which].astype(F32)
            high = result.astype(BF16)
            low = (result - high.astype(F32)).astype(BF16)
            both = jnp.dot(jnp.concatenate([high, low], axis=0), values, preferred_element_type=F32)
            both = both[:nf] + both[nf:]
            for e, number in enumerate(numbers):
                part = both[:, e * rows : (e + 1) * rows]
                for b in range(ab):
                    totals[b] = totals[b] + jnp.where(number == float(b), part, 0.0)
    for b in range(ab):
        image[:, b * rows : (b + 1) * rows] = totals[b]
    for k in range(n):
        start = k * per // rows * rows
        shift = k * per - start
        wide = (per + shift + rows - 1) // rows * rows

        @pl.when(c == k)
        def _():
            piece = image[:, start : start + wide]
            if shift:
                piece = pltpu.roll(piece, wide - shift, 1)
            out[...] = piece[:, :per]


def dense_kernel(n, ab, rows, *refs):
    own_c, own_r, left, right = refs[:n], refs[n : 2 * n], refs[2 * n], refs[2 * n + 1]
    r, c = lax.axis_index("row"), lax.axis_index("col")
    eye = lax.broadcasted_iota(jnp.int32, (rows, rows), 0) == lax.broadcasted_iota(jnp.int32, (rows, rows), 1)
    for blocks, out, places, weighted in (
        (own_c, right, col_places(n, r), True),
        (own_r, left, row_places(n, r, c), False),
    ):
        for block, place in zip(blocks, places):
            base = place * (2 * rows)
            for which in range(2):
                weight, numbers = info(block, rows, which)
                values = block[which * rows : (which + 1) * rows, :]
                if weighted:
                    scale = jnp.where(eye, jnp.broadcast_to(weight, (rows, rows)), 0.0).astype(BF16)
                    values = jnp.dot(scale, values, preferred_element_type=F32)
                else:
                    values = values.astype(F32)
                at = pl.ds(pl.multiple_of(base + which * rows, rows), rows)
                for b in range(ab):
                    total = jnp.zeros((rows, rows), F32)
                    for e, number in enumerate(numbers):
                        total = jnp.where(number == float(b), values[:, e * rows : (e + 1) * rows], total)
                    out[at, b * rows : (b + 1) * rows] = total.astype(BF16)


def shards(n, slope_matrix, prior_matrix, slope_blocks, prior_blocks, weight_ids, valid_mask, noise_weights, prior_weights, frames):
    rows, width = slope_matrix.shape
    per, nf = frames.shape
    ab = per * n // rows
    packed, sent = pl.pallas_call(
        functools.partial(pack_kernel, ab),
        out_shape=(
            pltpu.VMEM((2 * rows + EXTRA, width), BF16),
            pltpu.VMEM((nf, width), BF16),
        ),
        in_specs=[VMEM, VMEM, SMEM, SMEM, VMEM, VMEM, VMEM, SMEM, VMEM],
        out_specs=(VMEM, VMEM),
        name="pack",
    )(
        slope_matrix,
        prior_matrix,
        slope_blocks,
        prior_blocks,
        weight_ids[None, :],
        valid_mask[None, :],
        prior_weights[None, :],
        noise_weights,
        frames.T,
    )
    half = n // 2
    firsts = [permute(packed, n, lambda r, c, m=m: ((c + 2 * (m + r)) % n, r)) for m in range(half)]
    row_side = firsts + [permute(firsts[m], n, lambda r, c: (r, c ^ 1)) for m in range(half)]
    col_side = [packed, permute(packed, n, lambda r, c: (r ^ 1, c))]
    for m in range(1, half):
        other = permute(packed, n, lambda r, c, m=m: ((r + 2 * m) % n, c))
        col_side += [other, permute(other, n, lambda r, c: (r ^ 1, c))]
    mine = [sent] + [permute(sent, n, lambda r, c, k=k: (r, (c + k) % n)) for k in range(1, n)]
    picture = pl.pallas_call(
        functools.partial(picture_kernel, n, ab, rows, per),
        out_shape=pltpu.VMEM((2 * n, nf, rows), BF16),
        in_specs=[VMEM] * (2 * n),
        out_specs=VMEM,
        scratch_shapes=[pltpu.VMEM((nf, ab * rows), F32), pltpu.VMEM((n, nf, width), F32)],
        compiler_params=SMALL,
        name="picture",
    )(*here(*row_side, *mine))
    partner = permute(picture, n, lambda r, c: (r ^ 1, c))
    chip = (picture.astype(F32) + partner.astype(F32)).astype(BF16)
    sums = [chip] + [permute(chip, n, lambda r, c, m=m: ((r + 2 * m) % n, c)) for m in range(1, half)]
    applied = pl.pallas_call(
        functools.partial(applied_kernel, n, ab, rows, per),
        out_shape=jax.ShapeDtypeStruct((nf, per), F32),
        in_specs=[VMEM] * (n + half),
        out_specs=VMEM,
        scratch_shapes=[pltpu.VMEM((nf, ab * rows), F32)],
        compiler_params=SMALL,
        name="applied",
    )(*here(*row_side, *sums))
    left, right = pl.pallas_call(
        functools.partial(dense_kernel, n, ab, rows),
        out_shape=(pltpu.VMEM((2 * rows * n, ab * rows), BF16), pltpu.VMEM((2 * rows * n, ab * rows), BF16)),
        in_specs=[VMEM] * (2 * n),
        out_specs=(VMEM, VMEM),
        compiler_params=SMALL,
        name="dense",
    )(*here(*col_side, *row_side))
    gram = lax.dot_general(left, right, (((0,), (0,)), ((), ())), preferred_element_type=F32)
    return gram, applied.T


def solution(mesh):
    n = mesh.shape["row"]
    block = P(("groups", "row"), "col")
    line = P(("groups", "row"))
    whole = P(("groups", "row", "col"), None)
    in_specs = (block, block, block, block, line, line, P("groups"), line, whole)
    return jax.shard_map(
        functools.partial(shards, n), mesh=mesh, in_specs=in_specs, out_specs=(block, whole), check_vma=False
    )
```

```python
import functools

import jax
import jax.numpy as jnp
from jax import lax
from jax.experimental import pallas as pl
from jax.experimental.pallas import tpu as pltpu
from jax.sharding import PartitionSpec as P


VMEM = pl.BlockSpec(memory_space=pltpu.VMEM)
SMEM = pl.BlockSpec(memory_space=pltpu.SMEM)
F32 = jnp.float32
BF16 = jnp.bfloat16
EXTRA = 16
SMALL = pltpu.CompilerParams(vmem_limit_bytes=16 << 20)


def here(*values):
    return [pltpu.with_memory_space_constraint(v, pltpu.VMEM) for v in values]


def permute(value, n, source):
    pairs = []
    for r in range(n):
        for c in range(n):
            sr, sc = source(r, c)
            pairs.append((sr * n + sc, r * n + c))
    return lax.ppermute(value, ("row", "col"), pairs)


def pack_kernel(ab, slope, prior, ids_s, ids_p, wid, valid, pw, noise, frames, packed, sent):
    rows, width = slope.shape
    half = wid.shape[1]
    packed[0:rows, :] = slope[...]
    packed[rows : 2 * rows, :] = prior[...]
    picked = jnp.zeros((1, half), F32)
    for k in range(noise.shape[0]):
        picked = picked + jnp.where(wid[...] == k, noise[k], 0.0)
    picked = picked * valid[...].astype(F32)
    source = lax.broadcasted_iota(jnp.int32, (half, rows), 0)
    target = lax.broadcasted_iota(jnp.int32, (half, rows), 1)
    spread = jnp.where(target // 2 == source, 1.0, 0.0).astype(BF16)
    eight = jnp.broadcast_to(picked, (8, half)).astype(BF16)
    slope_w = jnp.dot(eight, spread, preferred_element_type=F32)[0:1]
    weights = jnp.concatenate([slope_w, pw[...].astype(F32)], axis=1)
    base = lax.axis_index("col") * ab
    row = lax.broadcasted_iota(jnp.int32, (EXTRA, width), 0)
    lane = lax.broadcasted_iota(jnp.int32, (EXTRA, width), 1)
    tile = jnp.where(row == 0, jnp.broadcast_to(weights, (EXTRA, width)), 0.0)
    for line, ids in ((1, ids_s), (2, ids_p)):
        for e in range(ids.shape[1]):
            here = (row == line) & (lane // rows == e)
            tile = jnp.where(here, (ids[0, e] - base).astype(F32), tile)
    packed[2 * rows :, :] = tile.astype(BF16)
    nf, per = frames.shape
    sent[...] = jnp.concatenate([frames[...], jnp.zeros((nf, width - per), F32)], axis=1).astype(BF16)


def info(block, rows, which):
    tile = block[2 * rows : 2 * rows + EXTRA, :].astype(F32)
    weight = tile[0:1, which * rows : (which + 1) * rows]
    numbers = [tile[1 + which : 2 + which, e * rows : (e + 1) * rows] for e in range(tile.shape[1] // rows)]
    return weight, numbers


def col_places(n, r):
    return [lax.rem((r ^ odd) + 2 * m, n) for m in range(n // 2) for odd in (0, 1)]


def row_places(n, r, c):
    return [lax.rem((c ^ 1 ^ odd) + 2 * (m + r), n) for odd in (0, 1) for m in range(n // 2)]


def picture_kernel(n, ab, rows, per, *refs):
    blocks, frames, out, image, slices = refs[:n], refs[n], refs[-3], refs[-2], refs[-1]
    r, c = lax.axis_index("row"), lax.axis_index("col")
    nf = frames.shape[0] // n
    for k in range(n):
        slices[c ^ k] = frames[k * nf : (k + 1) * nf, :].astype(F32)
    image[...] = jnp.zeros_like(image)
    for k in range(n):
        start = k * per // rows * rows
        shift = k * per - start
        wide = (per + shift + rows - 1) // rows * rows
        piece = slices[k]
        if shift:
            piece = pltpu.roll(piece, shift, 1)
        image[:, start : start + wide] += piece[:, :wide]
    parts = [image[:, b * rows : (b + 1) * rows] for b in range(ab)]
    for block, place in zip(blocks, row_places(n, r, c)):
        for which in range(2):
            weight, numbers = info(block, rows, which)
            chosen = []
            for number in numbers:
                pick = jnp.zeros((nf, rows), F32)
                for b in range(ab):
                    pick = jnp.where(number == float(b), parts[b], pick)
                chosen.append(pick)
            picked = jnp.concatenate(chosen, axis=1).astype(BF16)
            values = block[which * rows : (which + 1) * rows, :]
            result = lax.dot_general(picked, values, (((1,), (1,)), ((), ())), preferred_element_type=F32)
            out[2 * place + which] = (result * weight).astype(BF16)


def applied_kernel(n, rows, per, *refs):
    blocks, sums, out = refs[:n], refs[n : n + n // 2], refs[-1]
    r, c = lax.axis_index("row"), lax.axis_index("col")
    nf = out.shape[0]
    count = (per + rows - 1 + rows - 1) // rows
    first = c * per // rows
    wanted = [(first + k).astype(F32) for k in range(count)]
    totals = [jnp.zeros((nf, rows), F32) for _ in range(count)]
    for block, place in zip(blocks, row_places(n, r, c)):
        for which in range(2):
            _, numbers = info(block, rows, which)
            values = block[which * rows : (which + 1) * rows, :]
            result = sums[0][2 * place + which].astype(F32)
            for other in sums[1:]:
                result = result + other[2 * place + which].astype(F32)
            high = result.astype(BF16)
            low = (result - high.astype(F32)).astype(BF16)
            both = jnp.dot(jnp.concatenate([high, low], axis=0), values, preferred_element_type=F32)
            both = both[:nf] + both[nf:]
            for e, number in enumerate(numbers):
                part = both[:, e * rows : (e + 1) * rows]
                for k in range(count):
                    totals[k] = totals[k] + jnp.where(number == wanted[k], part, 0.0)
    image = jnp.concatenate(totals, axis=1)
    image = pltpu.roll(image, lax.rem(count * rows - (c * per - first * rows), count * rows), 1)
    out[...] = image[:, :per]


def dense_kernel(n, ab, rows, *refs):
    own_c, own_r, left, right = refs[:n], refs[n : 2 * n], refs[2 * n], refs[2 * n + 1]
    r, c = lax.axis_index("row"), lax.axis_index("col")
    eye = lax.broadcasted_iota(jnp.int32, (rows, rows), 0) == lax.broadcasted_iota(jnp.int32, (rows, rows), 1)
    for blocks, out, places, weighted in (
        (own_c, right, col_places(n, r), True),
        (own_r, left, row_places(n, r, c), False),
    ):
        for block, place in zip(blocks, places):
            base = place * (2 * rows)
            for which in range(2):
                weight, numbers = info(block, rows, which)
                values = block[which * rows : (which + 1) * rows, :]
                if weighted:
                    scale = jnp.where(eye, jnp.broadcast_to(weight, (rows, rows)), 0.0).astype(BF16)
                    values = jnp.dot(scale, values, preferred_element_type=F32)
                else:
                    values = values.astype(F32)
                at = pl.ds(pl.multiple_of(base + which * rows, rows), rows)
                for b in range(ab):
                    total = jnp.zeros((rows, rows), F32)
                    for e, number in enumerate(numbers):
                        total = jnp.where(number == float(b), values[:, e * rows : (e + 1) * rows], total)
                    out[at, b * rows : (b + 1) * rows] = total.astype(BF16)


def shards(n, slope_matrix, prior_matrix, slope_blocks, prior_blocks, weight_ids, valid_mask, noise_weights, prior_weights, frames):
    rows, width = slope_matrix.shape
    per, nf = frames.shape
    ab = per * n // rows
    packed, sent = pl.pallas_call(
        functools.partial(pack_kernel, ab),
        out_shape=(
            pltpu.VMEM((2 * rows + EXTRA, width), BF16),
            pltpu.VMEM((nf, width), BF16),
        ),
        in_specs=[VMEM, VMEM, SMEM, SMEM, VMEM, VMEM, VMEM, SMEM, VMEM],
        out_specs=(VMEM, VMEM),
        name="pack",
    )(
        slope_matrix,
        prior_matrix,
        slope_blocks,
        prior_blocks,
        weight_ids[None, :],
        valid_mask[None, :],
        prior_weights[None, :],
        noise_weights,
        frames.T,
    )
    half = n // 2
    firsts = [permute(packed, n, lambda r, c, m=m: (((c ^ 1) + 2 * (m + r)) % n, r)) for m in range(half)]
    row_side = firsts + [permute(firsts[m], n, lambda r, c: (r, c ^ 1)) for m in range(half)]
    col_side = [packed, permute(packed, n, lambda r, c: (r ^ 1, c))]
    for m in range(1, half):
        other = permute(packed, n, lambda r, c, m=m: ((r + 2 * m) % n, c))
        col_side += [other, permute(other, n, lambda r, c: (r ^ 1, c))]
    mine = sent
    for bit in range(n.bit_length() - 1):
        other = permute(mine, n, lambda r, c, bit=bit: (r, c ^ (1 << bit)))
        mine = jnp.concatenate([mine, other], axis=0)
    picture = pl.pallas_call(
        functools.partial(picture_kernel, n, ab, rows, per),
        out_shape=pltpu.VMEM((2 * n, nf, rows), BF16),
        in_specs=[VMEM] * (n + 1),
        out_specs=VMEM,
        scratch_shapes=[pltpu.VMEM((nf, ab * rows), F32), pltpu.VMEM((n, nf, width), F32)],
        compiler_params=SMALL,
        name="picture",
    )(*here(*row_side, mine))
    partner = permute(picture, n, lambda r, c: (r ^ 1, c))
    chip = (picture.astype(F32) + partner.astype(F32)).astype(BF16)
    sums = [chip] + [permute(chip, n, lambda r, c, m=m: ((r + 2 * m) % n, c)) for m in range(1, half)]
    applied = pl.pallas_call(
        functools.partial(applied_kernel, n, rows, per),
        out_shape=jax.ShapeDtypeStruct((nf, per), F32),
        in_specs=[VMEM] * (n + half),
        out_specs=VMEM,
        compiler_params=SMALL,
        name="applied",
    )(*here(*row_side, *sums))
    expand = pl.pallas_call(
        functools.partial(dense_kernel, n, ab, rows),
        out_shape=(pltpu.VMEM((2 * rows * n, ab * rows), BF16), pltpu.VMEM((2 * rows * n, ab * rows), BF16)),
        in_specs=[VMEM] * (2 * n),
        out_specs=(VMEM, VMEM),
        compiler_params=SMALL,
        name="dense",
    )
    left, right = expand(*here(*col_side, *row_side))
    gram = lax.dot_general(left, right, (((0,), (0,)), ((), ())), preferred_element_type=F32)
    return gram, applied.T


def solution(mesh):
    n = mesh.shape["row"]
    block = P(("groups", "row"), "col")
    line = P(("groups", "row"))
    whole = P(("groups", "row", "col"), None)
    in_specs = (block, block, block, block, line, line, P("groups"), line, whole)
    return jax.shard_map(
        functools.partial(shards, n), mesh=mesh, in_specs=in_specs, out_specs=(block, whole), check_vma=False
    )
```

```python
import functools

import jax
import jax.numpy as jnp
from jax import lax
from jax.experimental import pallas as pl
from jax.experimental.pallas import tpu as pltpu
from jax.sharding import PartitionSpec as P


VMEM = pl.BlockSpec(memory_space=pltpu.VMEM)
SMEM = pl.BlockSpec(memory_space=pltpu.SMEM)
F32 = jnp.float32
BF16 = jnp.bfloat16
EXTRA = 16
SMALL = pltpu.CompilerParams(vmem_limit_bytes=16 << 20)


def here(*values):
    return [pltpu.with_memory_space_constraint(v, pltpu.VMEM) for v in values]


def permute(value, n, source):
    pairs = []
    for r in range(n):
        for c in range(n):
            sr, sc = source(r, c)
            pairs.append((sr * n + sc, r * n + c))
    return lax.ppermute(value, ("row", "col"), pairs)


def pack_kernel(ab, slope, prior, ids_s, ids_p, wid, valid, pw, noise, frames, packed, sent):
    rows, width = slope.shape
    half = wid.shape[1]
    packed[0:rows, :] = slope[...]
    packed[rows : 2 * rows, :] = prior[...]
    picked = jnp.zeros((1, half), F32)
    for k in range(noise.shape[0]):
        picked = picked + jnp.where(wid[...] == k, noise[k], 0.0)
    picked = picked * valid[...].astype(F32)
    source = lax.broadcasted_iota(jnp.int32, (half, rows), 0)
    target = lax.broadcasted_iota(jnp.int32, (half, rows), 1)
    spread = jnp.where(target // 2 == source, 1.0, 0.0).astype(BF16)
    eight = jnp.broadcast_to(picked, (8, half)).astype(BF16)
    slope_w = jnp.dot(eight, spread, preferred_element_type=F32)[0:1]
    weights = jnp.concatenate([slope_w, pw[...].astype(F32)], axis=1)
    base = lax.axis_index("col") * ab
    row = lax.broadcasted_iota(jnp.int32, (EXTRA, width), 0)
    lane = lax.broadcasted_iota(jnp.int32, (EXTRA, width), 1)
    tile = jnp.where(row == 0, jnp.broadcast_to(weights, (EXTRA, width)), 0.0)
    for line, ids in ((1, ids_s), (2, ids_p)):
        for e in range(ids.shape[1]):
            here = (row == line) & (lane // rows == e)
            tile = jnp.where(here, (ids[0, e] - base).astype(F32), tile)
    packed[2 * rows :, :] = tile.astype(BF16)
    nf, per = frames.shape
    sent[...] = jnp.concatenate([frames[...], jnp.zeros((nf, width - per), F32)], axis=1).astype(BF16)


def info(block, rows, which):
    tile = block[2 * rows : 2 * rows + EXTRA, :].astype(F32)
    weight = tile[0:1, which * rows : (which + 1) * rows]
    numbers = [tile[1 + which : 2 + which, e * rows : (e + 1) * rows] for e in range(tile.shape[1] // rows)]
    return weight, numbers


def col_places(n, r):
    return [lax.rem((r ^ odd ^ min(m, 1)) + 2 * m, n) for m in range(n // 2) for odd in (0, 1)]


def row_places(n, r, c):
    return [lax.rem((c ^ odd ^ 1) + 2 * (m + r), n) for odd in (0, 1) for m in range(n // 2)]


def picture_kernel(n, ab, rows, per, *refs):
    blocks, frames, out, image, slices = refs[:n], refs[n], refs[-3], refs[-2], refs[-1]
    r, c = lax.axis_index("row"), lax.axis_index("col")
    nf = frames.shape[0] // n
    for k in range(n):
        slices[c ^ k] = frames[k * nf : (k + 1) * nf, :].astype(F32)
    image[...] = jnp.zeros_like(image)
    for k in range(n):
        start = k * per // rows * rows
        shift = k * per - start
        wide = (per + shift + rows - 1) // rows * rows
        piece = slices[k]
        if shift:
            piece = pltpu.roll(piece, shift, 1)
        image[:, start : start + wide] += piece[:, :wide]
    parts = [image[:, b * rows : (b + 1) * rows] for b in range(ab)]
    for block, place in zip(blocks, row_places(n, r, c)):
        for which in range(2):
            weight, numbers = info(block, rows, which)
            chosen = []
            for number in numbers:
                pick = jnp.zeros((nf, rows), F32)
                for b in range(ab):
                    pick = jnp.where(number == float(b), parts[b], pick)
                chosen.append(pick)
            picked = jnp.concatenate(chosen, axis=1).astype(BF16)
            values = block[which * rows : (which + 1) * rows, :]
            result = lax.dot_general(picked, values, (((1,), (1,)), ((), ())), preferred_element_type=F32)
            out[2 * place + which] = (result * weight).astype(BF16)


def applied_kernel(n, rows, per, *refs):
    blocks, sums, out = refs[:n], refs[n : n + n // 2], refs[-1]
    r, c = lax.axis_index("row"), lax.axis_index("col")
    nf = out.shape[0]
    count = (per + rows - 1 + rows - 1) // rows
    first = c * per // rows
    wanted = [(first + k).astype(F32) for k in range(count)]
    totals = [jnp.zeros((nf, rows), F32) for _ in range(count)]
    for block, place in zip(blocks, row_places(n, r, c)):
        for which in range(2):
            _, numbers = info(block, rows, which)
            values = block[which * rows : (which + 1) * rows, :]
            result = sums[0][2 * place + which].astype(F32)
            for other in sums[1:]:
                result = result + other[2 * place + which].astype(F32)
            high = result.astype(BF16)
            low = (result - high.astype(F32)).astype(BF16)
            both = jnp.dot(jnp.concatenate([high, low], axis=0), values, preferred_element_type=F32)
            both = both[:nf] + both[nf:]
            for e, number in enumerate(numbers):
                part = both[:, e * rows : (e + 1) * rows]
                for k in range(count):
                    totals[k] = totals[k] + jnp.where(number == wanted[k], part, 0.0)
    image = jnp.concatenate(totals, axis=1)
    image = pltpu.roll(image, lax.rem(count * rows - (c * per - first * rows), count * rows), 1)
    out[...] = image[:, :per]


def dense_kernel(n, ab, rows, *refs):
    own_c, own_r, left, right = refs[:n], refs[n : 2 * n], refs[2 * n], refs[2 * n + 1]
    r, c = lax.axis_index("row"), lax.axis_index("col")
    eye = lax.broadcasted_iota(jnp.int32, (rows, rows), 0) == lax.broadcasted_iota(jnp.int32, (rows, rows), 1)
    for blocks, out, places, weighted in (
        (own_c, right, col_places(n, r), True),
        (own_r, left, row_places(n, r, c), False),
    ):
        for block, place in zip(blocks, places):
            base = place * (2 * rows)
            for which in range(2):
                weight, numbers = info(block, rows, which)
                values = block[which * rows : (which + 1) * rows, :]
                if weighted:
                    scale = jnp.where(eye, jnp.broadcast_to(weight, (rows, rows)), 0.0).astype(BF16)
                    values = jnp.dot(scale, values, preferred_element_type=F32)
                else:
                    values = values.astype(F32)
                at = pl.ds(pl.multiple_of(base + which * rows, rows), rows)
                for b in range(ab):
                    total = jnp.zeros((rows, rows), F32)
                    for e, number in enumerate(numbers):
                        total = jnp.where(number == float(b), values[:, e * rows : (e + 1) * rows], total)
                    out[at, b * rows : (b + 1) * rows] = total.astype(BF16)


def shards(n, slope_matrix, prior_matrix, slope_blocks, prior_blocks, weight_ids, valid_mask, noise_weights, prior_weights, frames):
    rows, width = slope_matrix.shape
    per, nf = frames.shape
    ab = per * n // rows
    packed, sent = pl.pallas_call(
        functools.partial(pack_kernel, ab),
        out_shape=(
            pltpu.VMEM((2 * rows + EXTRA, width), BF16),
            pltpu.VMEM((nf, width), BF16),
        ),
        in_specs=[VMEM, VMEM, SMEM, SMEM, VMEM, VMEM, VMEM, SMEM, VMEM],
        out_specs=(VMEM, VMEM),
        name="pack",
    )(
        slope_matrix,
        prior_matrix,
        slope_blocks,
        prior_blocks,
        weight_ids[None, :],
        valid_mask[None, :],
        prior_weights[None, :],
        noise_weights,
        frames.T,
    )
    half = n // 2
    firsts = [permute(packed, n, lambda r, c, m=m: (((c ^ 1) + 2 * (m + r)) % n, r)) for m in range(half)]
    row_side = firsts + [permute(firsts[m], n, lambda r, c: (r, c ^ 1)) for m in range(half)]
    col_side = [packed, permute(packed, n, lambda r, c: (r ^ 1, c))]
    for m in range(1, half):
        other = permute(packed, n, lambda r, c, m=m: (((r ^ 1) + 2 * m) % n, c))
        col_side += [other, permute(other, n, lambda r, c: (r ^ 1, c))]
    mine = sent
    for bit in range(n.bit_length() - 1):
        other = permute(mine, n, lambda r, c, bit=bit: (r, c ^ (1 << bit)))
        mine = jnp.concatenate([mine, other], axis=0)
    picture = pl.pallas_call(
        functools.partial(picture_kernel, n, ab, rows, per),
        out_shape=pltpu.VMEM((2 * n, nf, rows), BF16),
        in_specs=[VMEM] * (n + 1),
        out_specs=VMEM,
        scratch_shapes=[pltpu.VMEM((nf, ab * rows), F32), pltpu.VMEM((n, nf, width), F32)],
        compiler_params=SMALL,
        name="picture",
    )(*here(*row_side, mine))
    partner = permute(picture, n, lambda r, c: (r ^ 1, c))
    chip = (picture.astype(F32) + partner.astype(F32)).astype(BF16)
    sums = [chip] + [permute(chip, n, lambda r, c, m=m: (((r ^ 1) + 2 * m) % n, c)) for m in range(1, half)]
    applied = pl.pallas_call(
        functools.partial(applied_kernel, n, rows, per),
        out_shape=jax.ShapeDtypeStruct((nf, per), F32),
        in_specs=[VMEM] * (n + half),
        out_specs=VMEM,
        compiler_params=SMALL,
        name="applied",
    )(*here(*row_side, *sums))
    expand = pl.pallas_call(
        functools.partial(dense_kernel, n, ab, rows),
        out_shape=(pltpu.VMEM((2 * rows * n, ab * rows), BF16), pltpu.VMEM((2 * rows * n, ab * rows), BF16)),
        in_specs=[VMEM] * (2 * n),
        out_specs=(VMEM, VMEM),
        compiler_params=SMALL,
        name="dense",
    )
    left, right = expand(*here(*col_side, *row_side))
    gram = lax.dot_general(left, right, (((0,), (0,)), ((), ())), preferred_element_type=F32)
    return gram, applied.T


def solution(mesh):
    n = mesh.shape["row"]
    block = P(("groups", "row"), "col")
    line = P(("groups", "row"))
    whole = P(("groups", "row", "col"), None)
    in_specs = (block, block, block, block, line, line, P("groups"), line, whole)
    return jax.shard_map(
        functools.partial(shards, n), mesh=mesh, in_specs=in_specs, out_specs=(block, whole), check_vma=False
    )
```
